32 devices in a mesh: freq: 4 (over y, x), clus: 8 (over z, core).
Axes of the slice: x: 2, y: 2, z: 4, core: 2. Of those that a mesh axis runs over, the one named last changes fastest.
Arguments:
- history: bfloat16 [1024, 8, 1024], P('freq', None, 'clus'), may hold values from -6 to 6
- near_blocks: bfloat16 [8, 4, 512, 2, 128, 128], P('clus', None, 'freq'), may hold values from -0.1875 to 0.1875
- near_list: int32 [8, 4], replicated, may hold values from 0 to 7, as said below
- basis_out: bfloat16 [512, 2, 32, 1024], P('freq', None, None, 'clus'), may hold values from -0.75 to 0.75
- basis_in: bfloat16 [512, 2, 32, 1024], P('freq', None, None, 'clus'), may hold values from -0.375 to 0.375
- coupling: bfloat16 [8, 512, 2, 32, 256], P('clus', 'freq'), may hold values from -0.375 to 0.375
- ranks: int32 [8, 512, 8], P('clus', 'freq'), may hold values from 4 to 32
Outputs:
- potential: bfloat16 [512, 2, 8, 1024], P('freq', None, None, 'clus')
The draws below stay inside these ranges and needn't reach their ends.
Inputs may be any that keep to these rules, and one draw needn't show every extreme that they name: `near_list`: row t starts with t itself; its other 3 entries are distinct shards other than t, each (t + d) mod 8 for some d with 1 <= |d| <= 3.
All inputs are finite; a program needn't handle non-finite values.
Results may differ from the reference program's by a relative error of at most 0.0055.
Values may be sent and summed in bfloat16 or wider, within the bound.
A program may use at most 128 MiB of HBM per device.

```python
import math
import jax
import jax.numpy as jnp
from jax import lax

STEPS = 1024
WAVES = 512
EXC = 8
PC = 128
NEAR = 4
RANK = 32
NPAN = 1024
N_CLUS = 8


def draw_near_list(key, part):
    reach = NEAR - 1

    def one_row(target):
        order = jax.random.permutation(jax.random.fold_in(key, target), 2 * reach)[:reach].astype(jnp.int32)
        offsets = jnp.where(order < reach, order + 1, reach - 1 - order)
        others = (target + offsets + N_CLUS) % N_CLUS
        return jnp.concatenate([jnp.reshape(target, (1,)).astype(jnp.int32), others.astype(jnp.int32)])
    return jax.vmap(one_row)(lax.iota(jnp.int32, N_CLUS))


def place_ends(drawn, own_key, smallest, top_value):
    longest = drawn.shape.index(max(drawn.shape))
    spots = []
    for shift in (0, 1):
        where = [jax.random.randint(jax.random.fold_in(own_key, axis), (), 0, length) for axis, length in enumerate(drawn.shape)]
        where[longest] = (where[longest] + shift) % drawn.shape[longest]
        spots.append(tuple(where))
    return drawn.at[spots[0]].set(smallest).at[spots[1]].set(top_value)


def shard_levels(stream_key, dims, pieces, least, largest):
    gain = 1.0
    for axis_at, blocks in pieces:
        draws = jax.random.uniform(jax.random.fold_in(jax.random.fold_in(stream_key, 6), axis_at), (blocks,), jnp.float32, least / len(pieces), largest / len(pieces))
        gain = gain * jnp.repeat(jnp.exp(draws), dims[axis_at] // blocks).reshape((-1,) + (1,) * (len(dims) - 1 - axis_at))
    return gain


def centred(rng, extent, deviation, most, cuts=(), held_as=jnp.bfloat16):
    entries = deviation * jax.random.normal(rng, extent, jnp.float32)
    if cuts:
        entries = entries * shard_levels(rng, extent, cuts, -0.22, 0.18)
    return jnp.clip(entries, -most, most).astype(held_as)


def setup_inputs(seed: int = 0) -> dict:
    arg_keys = jax.random.split(jax.random.key(seed), 8)
    return {
        "history": centred(arg_keys[0], (STEPS, EXC, NPAN), 1.0, 6.0, ((0, 4), (2, 8))),
        "near_blocks": centred(arg_keys[1], (N_CLUS, NEAR, WAVES, 2, PC, PC), (2 * NEAR * PC) ** -0.5, 0.1875, ((0, 8), (2, 4))),
        "near_list": draw_near_list(jax.random.fold_in(arg_keys[7], 71), 0),
        "basis_out": centred(arg_keys[3], (WAVES, 2, RANK, NPAN), (2 * RANK) ** -0.5, 0.75, ((0, 4), (3, 8))),
        "basis_in": centred(arg_keys[4], (WAVES, 2, RANK, NPAN), (2 * PC) ** -0.5, 0.375, ((0, 4), (3, 8))),
        "coupling": centred(arg_keys[5], (N_CLUS, WAVES, 2, RANK, N_CLUS * RANK), (RANK * N_CLUS) ** -0.5, 0.375, ((0, 8), (1, 4))),
        "ranks": place_ends(jax.random.randint(arg_keys[6], (N_CLUS, WAVES, N_CLUS), RANK // 8, RANK + 1), jax.random.fold_in(arg_keys[6], 1), RANK // 8, RANK).astype(jnp.int32),
    }


def wave_table(first_wave, count, first_step, length, total):
    waves = first_wave + lax.iota(jnp.int32, count)
    steps = first_step + lax.iota(jnp.int32, length)
    phase = (waves[:, None] * steps[None, :]) % total
    angle = phase.astype(jnp.float32) * (2.0 * math.pi / total)
    weight = jnp.exp(steps.astype(jnp.float32) * (-math.log(2.0) / total)) * (total ** -0.5)
    return weight[None, :] * jnp.cos(angle), -weight[None, :] * jnp.sin(angle)


def transform(history, cos_tab, sin_tab):
    flat = history.reshape(history.shape[0], -1).astype(jnp.float32)
    real_part = jnp.dot(cos_tab, flat, precision=lax.Precision.HIGHEST)
    imag_part = jnp.dot(sin_tab, flat, precision=lax.Precision.HIGHEST)
    return jnp.stack([real_part, imag_part], 1).reshape(cos_tab.shape[0], 2, history.shape[1], history.shape[2])


def complex_product(form, left_re, left_im, right_re, right_im):
    def product(left, right):
        return jnp.einsum(form, left.astype(jnp.float32), right.astype(jnp.float32))
    return product(left_re, right_re) - product(left_im, right_im), product(left_re, right_im) + product(left_im, right_re)


def far_mask(limit, nearby, clusters, rank):
    position = lax.iota(jnp.int32, rank)
    keep_out = position[None, None, :] < limit[:, :, None]
    keep_in = keep_out & jnp.logical_not(nearby)[None, :, None]
    mask = jnp.transpose(keep_out, (0, 2, 1))[:, :, :, None] & keep_in[:, None, :, :]
    return mask.reshape(limit.shape[0], rank, clusters * rank)


def reference(history, near_blocks, near_list, basis_out, basis_in, coupling, ranks):
    cos_tab, sin_tab = wave_table(0, WAVES, 0, STEPS, STEPS)
    dens = transform(history, cos_tab, sin_tab).astype(jnp.bfloat16)
    spaced = dens.reshape(WAVES, 2, EXC, N_CLUS, PC)
    basis = basis_in.reshape(WAVES, 2, RANK, N_CLUS, PC)
    coeff_re, coeff_im = complex_product("krsp,kesp->kesr", basis[:, 0], basis[:, 1], spaced[:, 0], spaced[:, 1])
    coeffs = jnp.stack([coeff_re, coeff_im], 1).astype(jnp.bfloat16)
    stacked = coeffs.reshape(WAVES, 2, EXC, N_CLUS * RANK)
    cluster_ids = lax.iota(jnp.int32, N_CLUS)
    outputs = []
    for target in range(N_CLUS):
        chosen = jnp.stack([lax.dynamic_slice_in_dim(dens, (near_list[target, slot] * PC).astype(jnp.int32), PC, 3) for slot in range(NEAR)])
        blocks = near_blocks[target]
        near_re, near_im = complex_product("jkpq,jkeq->kep", blocks[:, :, 0], blocks[:, :, 1], chosen[:, :, 0], chosen[:, :, 1])
        nearby = jnp.any(near_list[target][:, None] == cluster_ids[None, :], axis=0)
        mask = far_mask(ranks[target], nearby, N_CLUS, RANK)
        couple = coupling[target]
        couple_re = jnp.where(mask, couple[:, 0], jnp.zeros_like(couple[:, 0]))
        couple_im = jnp.where(mask, couple[:, 1], jnp.zeros_like(couple[:, 1]))
        mixed_re, mixed_im = complex_product("kim,kem->kei", couple_re, couple_im, stacked[:, 0], stacked[:, 1])
        mixed_re = mixed_re.astype(jnp.bfloat16)
        mixed_im = mixed_im.astype(jnp.bfloat16)
        out_basis = basis_out[:, :, :, target * PC:(target + 1) * PC]
        far_re, far_im = complex_product("kip,kei->kep", out_basis[:, 0], out_basis[:, 1], mixed_re, mixed_im)
        outputs.append(jnp.stack([near_re + far_re, near_im + far_im], 1).astype(jnp.bfloat16))
    return jnp.concatenate(outputs, axis=3)
```

```python
import functools
import math

import jax
import jax.numpy as jnp
import numpy as np
from jax import lax
from jax.experimental import pallas as pl
from jax.experimental.pallas import tpu as pltpu
from jax.sharding import PartitionSpec as P

LANES = 128
NT = (((1,), (1,)), ((), ()))
NN = (((1,), (0,)), ((), ()))
MESH = pl.DeviceIdType.MESH
GROUP = 4
CUTS = (2, 4, 6, 7, 8)
LOADS = 4
PERIOD = 16


def dot(left, right, dims):
    return lax.dot_general(left, right, dims, preferred_element_type=jnp.float32)


def wave_constants(freqs, waves, total):
    rows = np.arange(2 * freqs * waves)
    wave, part = GROUP * (rows // (2 * GROUP)) + rows % GROUP, (rows // GROUP) % 2

    def factor(steps, scale):
        angle = (wave[:, None] * steps[None, :] % total) * (2.0 * math.pi / total)
        weight = np.exp(steps * (-math.log(2.0) / total)) * scale
        return weight * np.cos(angle), -weight * np.sin(angle)

    f_re, f_im = factor(np.arange(LANES), total ** (-0.5))
    imag = (part == 1)[:, None]
    fine = np.stack([np.where(imag, f_im, f_re), np.where(imag, f_re, -f_im)])
    fine = fine.reshape(2, freqs, 2 * waves, LANES).transpose(1, 0, 2, 3)
    c_re, c_im = factor(np.arange(total // LANES) * LANES, 1.0)
    coarse = np.stack([c_re[:PERIOD], c_im[:PERIOD]]).transpose(2, 0, 1)
    coarse = np.broadcast_to(coarse[..., None], coarse.shape + (LANES,))
    return jnp.asarray(fine, jnp.float32), jnp.asarray(coarse, jnp.float32)


def fill_tables(coarse, fine, table):
    spans, rows, half = coarse.shape[0], fine.shape[1], table.shape[1] // 2
    repeat = rows // PERIOD

    def step(a, carry):
        p = fine[0].reshape(repeat, PERIOD, LANES)
        q = fine[1].reshape(repeat, PERIOD, LANES)
        value = (coarse[a, 0] * p + coarse[a, 1] * q).reshape(rows, LANES)
        high = value.astype(jnp.bfloat16)
        low = (value - high.astype(jnp.float32)).astype(jnp.bfloat16)
        lanes = pl.ds(pl.multiple_of(a * LANES, LANES), LANES)
        for p in range(2):
            table[p, :half, lanes] = high[p * half : (p + 1) * half]
            table[p, half:, lanes] = low[p * half : (p + 1) * half]
        return carry

    lax.fori_loop(0, spans, step, 0)


def transform(g, p, hist, table):
    blocks, length = hist.shape[0], hist.shape[2]
    half = table.shape[1] // 2
    value = None
    for f in range(blocks):
        steps = jnp.concatenate([hist[f, 2 * g], hist[f, 2 * g + 1]], axis=1)
        term = dot(table[p, :, f * length : (f + 1) * length], steps, NN)
        value = term if value is None else value + term
    value = value[:half] + value[half:]
    one, two = [value[:, i * LANES : (i + 1) * LANES].reshape(-1, 2 * GROUP, LANES) for i in range(2)]
    upper = lax.broadcasted_iota(jnp.int32, one.shape, 1) < GROUP
    real = jnp.where(upper, one, pltpu.roll(two, GROUP, 1))
    imag = jnp.where(upper, pltpu.roll(one, GROUP, 1), two)
    return jnp.concatenate([real, imag], axis=1).astype(jnp.bfloat16)


def pairs_of(both, width):
    rows = 2 * GROUP
    re, im = both[:, :width], both[:, width:]
    real, imag = [], []
    for g in range(both.shape[0] // (2 * rows)):
        a, b = 2 * g * rows, (2 * g + 1) * rows
        real.append(re[a : a + rows] - im[b : b + rows])
        imag.append(re[b : b + rows] + im[a : a + rows])
    return jnp.concatenate(real, 0), jnp.concatenate(imag, 0)


def kernel(freqs, clusters, near_list, ranks, fine_in, coarse_in, own, near_in, couple_in, out_in, in_in,
           out, raw, wide, hist, fine, coarse, table, near, couple, basis_out, basis_in, limit, far, spread, *rest):
    parts = len(CUTS)
    pre = [rest[0:2], rest[2:4]]
    post = rest[4 : 4 + parts]
    packs = rest[4 + parts : 6 + parts]
    local_sem, near_sem, hist_send, hist_recv, send_sem, recv_sem = rest[6 + parts :]
    f, c = lax.axis_index("freq"), lax.axis_index("clus")
    z, core = c // 2, c % 2
    levels = clusters // 2
    has_up, has_down = z + 1 < levels, z > 0
    up, down, partner = c + 2, c - 2, c + 1 - 2 * core
    square = freqs == 4
    beside, across = f + 1 - 2 * (f % 2), (f + 2) % freqs
    peers = [beside, across] if square else [(f + i) % freqs for i in range(1, freqs)]
    slots, waves, panels = near.shape[0], near.shape[1], near.shape[3]
    exc, rank, sources = hist.shape[1], basis_in.shape[2], clusters
    blocks = waves // GROUP
    half = blocks // 2
    ends = [blocks * cut // CUTS[-1] for cut in CUTS]
    starts = [0] + ends[:-1]

    loads = [
        pltpu.make_async_copy(own, raw, local_sem.at[0]),
        pltpu.make_async_copy(fine_in.at[f], fine, local_sem.at[1]),
        pltpu.make_async_copy(coarse_in, coarse, local_sem.at[2]),
        pltpu.make_async_copy(in_in, basis_in, local_sem.at[3]),
        pltpu.make_async_copy(couple_in.at[0], couple, local_sem.at[4]),
        pltpu.make_async_copy(out_in, basis_out, local_sem.at[5]),
    ]
    share = waves // LOADS
    chunks = [
        pltpu.make_async_copy(
            near_in.at[0, :, pl.ds(w * share, share)], near.at[:, pl.ds(w * share, share)], near_sem.at[w]
        )
        for w in range(LOADS)
    ]

    barrier = pltpu.get_barrier_semaphore()
    for peer in peers:
        pl.semaphore_signal(barrier, inc=1, device_id=(peer, c), device_id_type=MESH)
    pl.semaphore_signal(barrier, inc=1, device_id=(f, partner), device_id_type=MESH)

    def when(flag, action):
        @pl.when(flag)
        def _():
            action()

    when(has_up, lambda: pl.semaphore_signal(barrier, inc=1, device_id=(f, up), device_id_type=MESH))
    when(has_down, lambda: pl.semaphore_signal(barrier, inc=1, device_id=(f, down), device_id_type=MESH))
    for copy in loads[:3]:
        copy.start()

    sent = []

    def give(peer, slot, e, number):
        return pltpu.make_async_remote_copy(
            src_ref=hist.at[slot, e], dst_ref=hist.at[slot, e],
            send_sem=hist_send.at[number, e], recv_sem=hist_recv.at[slot, e],
            device_id=(peer, c), device_id_type=MESH,
        )

    def arrived(slot, e):
        give(peers[0], slot, e, 0).wait_recv()

    def send(*what):
        sent.append(give(*what))
        sent[-1].start()

    def turn(g):
        for e in (2 * g, 2 * g + 1):
            hist[f, e] = wide[:, e, :].astype(jnp.bfloat16)

    def give_pair(g):
        for i in range(2):
            for number, peer in enumerate(peers):
                send(peer, f, 2 * g + (i + number) % 2, number)

    def relay_pair(g):
        if square:
            arrived(beside, 2 * g)
            send(across, beside, 2 * g, len(peers))
            arrived(across, 2 * g + 1)
            send(beside, across, 2 * g + 1, len(peers))

    def finish_pair(g):
        if square:
            corner = (beside + 2) % freqs
            order = [(beside, 1), (across, 0), (corner, 0), (corner, 1)]
        else:
            order = [(peer, part) for peer in peers for part in range(2)]
        for slot, part in order:
            arrived(slot, 2 * g + part)

    units = [pre[0][0], pre[0][1], pre[1][0], pre[1][1], packs[0], packs[1]] + list(post)

    def pass_on(u, source, target, way):
        return pltpu.make_async_remote_copy(
            src_ref=units[u].at[source], dst_ref=units[u].at[source],
            send_sem=send_sem.at[u, source // 2, way], recv_sem=recv_sem.at[u, source],
            device_id=(f, target), device_id_type=MESH,
        )

    state = {"own": 0, "tick": 0}

    def send_own():
        u = state["own"]
        when(has_up, lambda: pass_on(u, c, up, 0).start())
        when(has_down, lambda: pass_on(u, c, down, 1).start())
        pass_on(u, c, partner, 2).start()
        state["own"] += 1

    def relay(u, d):
        below, above = c - 2 * d, c + 2 * d

        def from_below():
            pass_on(u, below, partner, 2).wait_recv()
            when(has_up, lambda: pass_on(u, below, up, 0).start())
            pass_on(u, below, partner, 2).start()

        def from_above():
            pass_on(u, above, partner, 2).wait_recv()
            when(has_down, lambda: pass_on(u, above, down, 1).start())
            pass_on(u, above, partner, 2).start()

        when(z >= d, from_below)
        when(z + d < levels, from_above)

    def pump(tick):
        while state["tick"] < tick:
            state["tick"] += 1
            for d in range(levels - 1, 0, -1):
                u = state["tick"] - d
                if 0 <= u < len(units):
                    relay(u, d)

    def complete(u):
        pump(u + levels - 1)
        pass_on(u, partner, partner, 2).wait_recv()
        for d in range(1, levels):
            below, above = partner - 2 * d, partner + 2 * d
            when(z >= d, lambda: pass_on(u, below, partner, 2).wait_recv())
            when(z + d < levels, lambda: pass_on(u, above, partner, 2).wait_recv())

    def make(g, p):
        value = transform(g, p, hist, table)
        if g < 2:
            pre[g][p][c] = value
            return
        for w in range(parts):
            if p * half <= starts[w] < (p + 1) * half:
                post[w][c, g - 2] = value[starts[w] - p * half : ends[w] - p * half]

    def compress(w):
        p = starts[w] // half
        lane = lax.broadcasted_iota(jnp.int32, (exc, LANES), 1) // rank

        def step(i, carry):
            b = starts[w] - p * half + i
            left = jnp.concatenate([pre[0][p][c, b], pre[1][p][c, b], post[w][c, 0, i], post[w][c, 1, i]], 0)
            first = (starts[w] + i) * GROUP
            right = [basis_in[pl.ds(first, GROUP), part].reshape(GROUP * rank, panels) for part in range(2)]
            pair = pairs_of(dot(left, jnp.concatenate(right, 0), NT), GROUP * rank)
            outs = []
            for part in range(2):
                spread[part] = pair[part]
                rows = spread[part, pl.ds(0, exc, stride=GROUP), :]
                for k in range(1, GROUP):
                    rows = jnp.where(lane == k, spread[part, pl.ds(k, exc, stride=GROUP), :], rows)
                outs.append(rows)
            packs[p][c, b] = jnp.concatenate(outs, 0).astype(jnp.bfloat16)
            return carry

        lax.fori_loop(0, ends[w] - starts[w], step, 0)

    def set_limits():
        width = sources * rank
        source = lax.broadcasted_iota(jnp.int32, (sources, width), 1) // rank
        keep = source == lax.broadcasted_iota(jnp.int32, (sources, width), 0)
        for j in range(slots):
            keep = keep & (source != near_list[j, c])
        turned = jnp.transpose(ranks[...].astype(jnp.float32)).astype(jnp.bfloat16)
        top = dot(turned, jnp.where(keep, 1.0, 0.0).astype(jnp.bfloat16), NN)
        within = (lax.broadcasted_iota(jnp.int32, top.shape, 1) % rank).astype(jnp.float32)
        limit[...] = jnp.where(within < top, top, 0.0)

    def far_half(p):
        unroll = min(2, half)
        rows = 2 * exc
        position = lax.broadcasted_iota(jnp.int32, (rank, sources * rank), 0).astype(jnp.float32)

        def step(pair, carry):
            local = [pair * unroll + u for u in range(unroll)]
            members = [((p * half + b) * GROUP + i, i, u) for u, b in enumerate(local) for i in range(GROUP)]
            packed = [[packs[p][s, b].astype(jnp.float32) for s in range(sources)] for b in local]
            stacked = [
                jnp.concatenate([v[:, i * rank : (i + 1) * rank] for v in packed[u]], axis=1).astype(jnp.bfloat16)
                for _, i, u in members
            ]
            mixes = []
            for (wave, _, _), left in zip(members, stacked):
                keep = position < limit[pl.ds(wave, 1), :]
                views = [couple[wave, part] for part in range(2)]
                mixes.append([dot(left, jnp.where(keep, v, jnp.zeros_like(v)), NT) for v in views])
            mixed = [
                jnp.concatenate([r[:exc] - m[exc:], r[exc:] + m[:exc]], 0).astype(jnp.bfloat16) for r, m in mixes
            ]
            sums = [[dot(m, basis_out[wave, part], NN) for part in range(2)] for (wave, _, _), m in zip(members, mixed)]
            for (wave, _, _), (r, m) in zip(members, sums):
                far[wave, pl.ds(0, exc)] = r[:exc] - m[exc:]
                far[wave, pl.ds(exc, rows - exc)] = r[exc:] + m[:exc]
            return carry

        lax.fori_loop(0, half // unroll, step, 0)

    picked = [near_list[j, c] for j in range(slots)]

    def near_part(w):
        p = starts[w] // half
        mine = lax.broadcasted_iota(jnp.int32, (GROUP * exc, panels), 0) % GROUP

        def step(i, carry):
            b = starts[w] - p * half + i
            views = [[pre[0][p][s, b], pre[1][p][s, b], post[w][s, 0, i], post[w][s, 1, i]] for s in picked]
            left = jnp.concatenate([jnp.concatenate(v, 0) for v in views], 1)
            first = (starts[w] + i) * GROUP
            total = None
            for k in range(GROUP):
                right = [near[j, first + k].reshape(2 * panels, panels) for j in range(slots)]
                pair = pairs_of(dot(left, jnp.concatenate(right, 1), NT), panels)
                total = pair if total is None else [jnp.where(mine == k, v, t) for v, t in zip(pair, total)]
            for part in range(2):
                spread[part] = total[part]
            for k in range(GROUP):
                for part in range(2):
                    rows = spread[part, pl.ds(k, exc, stride=GROUP), :]
                    out[first + k, part] = (rows + far[first + k, pl.ds(part * exc, exc)]).astype(out.dtype)
            return carry

        lax.fori_loop(0, ends[w] - starts[w], step, 0)

    loads[0].wait()
    wide[...] = raw[...].astype(jnp.float32)
    turn(0)
    pl.semaphore_wait(barrier, len(peers) + 1 + jnp.where(z + 1 < levels, 1, 0) + jnp.where(z > 0, 1, 0))
    give_pair(0)
    for copy in loads[3:] + chunks:
        copy.start()
    for g in range(1, exc // 2):
        turn(g)
    for copy in loads[1:3]:
        copy.wait()
    fill_tables(coarse, fine, table)
    set_limits()

    last = exc // 2 - 1
    for g in range(exc // 2):
        relay_pair(g)
        if g < last:
            give_pair(g + 1)
        pump(min(2 * g - 1, 2 * len(pre)))
        finish_pair(g)
        for p in range(2):
            make(g, p)
            if g < 2:
                send_own()
    loads[3].wait()
    for w in range(parts):
        compress(w)
        if ends[w] % half == 0:
            send_own()
    pump(len(pre) * 2 + 1)
    send_own()
    pump(len(pre) * 2 + 2)
    send_own()
    for copy in loads[4:]:
        copy.wait()
    for p in range(2):
        complete(4 + p)
        far_half(p)
        send_own()
    while state["own"] < len(units):
        send_own()
    ready = 0
    for w in range(parts):
        if starts[w] % half == 0:
            for g in range(2):
                complete(2 * g + starts[w] // half)
        complete(6 + w)
        while ready < LOADS and ready * share < ends[w] * GROUP:
            chunks[ready].wait()
            ready += 1
        near_part(w)

    for copy in sent:
        copy.wait_send()
    for u in range(len(units)):
        when(has_up, lambda: pass_on(u, c, up, 0).wait_send())
        when(has_down, lambda: pass_on(u, c, down, 1).wait_send())
        pass_on(u, c, partner, 2).wait_send()
        for d in range(1, levels):
            below, above = c - 2 * d, c + 2 * d

            def below_sent():
                when(has_up, lambda: pass_on(u, below, up, 0).wait_send())
                pass_on(u, below, partner, 2).wait_send()

            def above_sent():
                when(has_down, lambda: pass_on(u, above, down, 1).wait_send())
                pass_on(u, above, partner, 2).wait_send()

            when(z >= d, below_sent)
            when(z + d < levels, above_sent)


def local(history, near_blocks, near_list, basis_out, basis_in, coupling, ranks):
    length, exc, panels = history.shape
    waves, _, rank, _ = basis_in.shape
    clusters = lax.axis_size("clus")
    freqs = lax.axis_size("freq")
    slots = near_blocks.shape[1]
    total = length * freqs
    blocks = waves // GROUP
    half = blocks // 2
    rows = 2 * exc
    bf16, f32 = jnp.bfloat16, jnp.float32
    fine, coarse = wave_constants(freqs, waves, total)
    ends = [blocks * cut // CUTS[-1] for cut in CUTS]
    sizes = [b - a for a, b in zip([0] + ends[:-1], ends)]
    vmem, anywhere = pl.BlockSpec(memory_space=pltpu.VMEM), pl.BlockSpec(memory_space=pl.ANY)
    dma = pltpu.SemaphoreType.DMA
    units = 6 + len(CUTS)
    return pl.pallas_call(
        functools.partial(kernel, freqs, clusters),
        out_shape=jax.ShapeDtypeStruct((waves, 2, exc, panels), bf16),
        in_specs=[pl.BlockSpec(memory_space=pltpu.SMEM), vmem] + [anywhere] * 7,
        out_specs=vmem,
        scratch_shapes=[
            pltpu.VMEM(history.shape, bf16),
            pltpu.VMEM(history.shape, f32),
            pltpu.VMEM((freqs, exc, length, panels), bf16),
            pltpu.VMEM(fine.shape[1:], f32),
            pltpu.VMEM(coarse.shape, f32),
            pltpu.VMEM((2, 2 * waves, total), bf16),
            pltpu.VMEM(near_blocks.shape[1:], bf16),
            pltpu.VMEM(coupling.shape[1:], bf16),
            pltpu.VMEM(basis_out.shape, bf16),
            pltpu.VMEM(basis_in.shape, bf16),
            pltpu.VMEM((waves, clusters * rank), f32),
            pltpu.VMEM((waves, rows, panels), f32),
            pltpu.VMEM((2, GROUP * exc, panels), f32),
        ]
        + [pltpu.VMEM((clusters, half, 4 * GROUP, panels), bf16)] * 4
        + [pltpu.VMEM((clusters, 2, size, 4 * GROUP, panels), bf16) for size in sizes]
        + [pltpu.VMEM((clusters, half, rows, GROUP * rank), bf16)] * 2
        + [
            dma((6,)),
            dma((LOADS,)),
            dma((freqs, exc)),
            dma((freqs, exc)),
            dma((units, clusters // 2, 3)),
            dma((units, clusters)),
        ],
        compiler_params=pltpu.CompilerParams(
            collective_id=0, has_side_effects=True, vmem_limit_bytes=60 * 1024 * 1024
        ),
    )(near_list.T, ranks[0].T, fine, coarse, history, near_blocks, coupling, basis_out, basis_in)


def solution(mesh):
    placed = (
        P("freq", None, "clus"),
        P("clus", None, "freq", None, None, None),
        P(),
        P("freq", None, None, "clus"),
        P("freq", None, None, "clus"),
        P("clus", "freq", None, None, None),
        P("clus", "freq", None),
    )
    return jax.shard_map(
        local, mesh=mesh, in_specs=placed, out_specs=P("freq", None, None, "clus"), check_vma=False
    )
```

```python
import functools
import math

import jax
import jax.numpy as jnp
import numpy as np
from jax import lax
from jax.experimental import pallas as pl
from jax.experimental.pallas import tpu as pltpu
from jax.sharding import PartitionSpec as P

LANES = 128
NT = (((1,), (1,)), ((), ()))
NN = (((1,), (0,)), ((), ()))
MESH = pl.DeviceIdType.MESH
GROUP = 4
CUTS = (2, 4, 6, 7, 8)
LOADS = 4
PERIOD = 16
UNROLL = 4
KEEP = 5


def dot(left, right, dims):
    return lax.dot_general(left, right, dims, preferred_element_type=jnp.float32)


def wave_constants(freqs, waves, total):
    rows = np.arange(2 * freqs * waves)
    wave, part = GROUP * (rows // (2 * GROUP)) + rows % GROUP, (rows // GROUP) % 2

    def factor(steps, scale):
        angle = (wave[:, None] * steps[None, :] % total) * (2.0 * math.pi / total)
        weight = np.exp(steps * (-math.log(2.0) / total)) * scale
        return weight * np.cos(angle), -weight * np.sin(angle)

    f_re, f_im = factor(np.arange(LANES), total ** (-0.5))
    imag = (part == 1)[:, None]
    fine = np.stack([np.where(imag, f_im, f_re), np.where(imag, f_re, -f_im)])
    fine = fine.reshape(2, freqs, 2 * waves, LANES).transpose(1, 0, 2, 3)
    c_re, c_im = factor(np.arange(total // LANES) * LANES, 1.0)
    coarse = np.stack([c_re[:PERIOD], c_im[:PERIOD]]).transpose(2, 0, 1)
    coarse = np.broadcast_to(coarse[..., None], coarse.shape + (LANES,))
    return jnp.asarray(fine, jnp.float32), jnp.asarray(coarse, jnp.float32)


def fill_tables(coarse, fine, table):
    spans, rows, half = coarse.shape[0], fine.shape[1], table.shape[1] // 2
    repeat = rows // PERIOD

    def step(a, carry):
        p = fine[0].reshape(repeat, PERIOD, LANES)
        q = fine[1].reshape(repeat, PERIOD, LANES)
        value = (coarse[a, 0] * p + coarse[a, 1] * q).reshape(rows, LANES)
        high = value.astype(jnp.bfloat16)
        low = (value - high.astype(jnp.float32)).astype(jnp.bfloat16)
        lanes = pl.ds(pl.multiple_of(a * LANES, LANES), LANES)
        for p in range(2):
            table[p, :half, lanes] = high[p * half : (p + 1) * half]
            table[p, half:, lanes] = low[p * half : (p + 1) * half]
        return carry

    lax.fori_loop(0, spans, step, 0)


def transform(g, p, hist, table):
    blocks, length = hist.shape[0], hist.shape[2]
    half = table.shape[1] // 2
    value = None
    for f in range(blocks):
        steps = jnp.concatenate([hist[f, 2 * g], hist[f, 2 * g + 1]], axis=1)
        term = dot(table[p, :, f * length : (f + 1) * length], steps, NN)
        value = term if value is None else value + term
    value = value[:half] + value[half:]
    one, two = [value[:, i * LANES : (i + 1) * LANES].reshape(-1, 2 * GROUP, LANES) for i in range(2)]
    upper = lax.broadcasted_iota(jnp.int32, one.shape, 1) < GROUP
    real = jnp.where(upper, one, pltpu.roll(two, GROUP, 1))
    imag = jnp.where(upper, pltpu.roll(one, GROUP, 1), two)
    return jnp.concatenate([real, imag], axis=1).astype(jnp.bfloat16)


def pairs_of(both, width):
    rows = 2 * GROUP
    re, im = both[:, :width], both[:, width:]
    real, imag = [], []
    for g in range(both.shape[0] // (2 * rows)):
        a, b = 2 * g * rows, (2 * g + 1) * rows
        real.append(re[a : a + rows] - im[b : b + rows])
        imag.append(re[b : b + rows] + im[a : a + rows])
    return jnp.concatenate(real, 0), jnp.concatenate(imag, 0)


def kernel(freqs, clusters, near_list, ranks, fine_in, coarse_in, own, near_in, couple_in, out_in, in_in,
           result, out, raw, wide, hist, fine, coarse, table, near, couple, basis_out, basis_in, limit, far, spread, *rest):
    parts = len(CUTS)
    pre = [rest[0:2], rest[2:4]]
    post = rest[4 : 4 + parts]
    local_sem, near_sem, out_sem, hist_send, hist_recv, send_sem, recv_sem = rest[4 + parts :]
    f, c = lax.axis_index("freq"), lax.axis_index("clus")
    z, core = c // 2, c % 2
    levels = clusters // 2
    has_up, has_down = z + 1 < levels, z > 0
    up, down, partner = c + 2, c - 2, c + 1 - 2 * core
    square = freqs == 4
    beside, across = f + 1 - 2 * (f % 2), (f + 2) % freqs
    peers = [beside, across] if square else [(f + i) % freqs for i in range(1, freqs)]
    slots, waves, panels = near.shape[0], near.shape[1], near.shape[3]
    exc, rank, sources = hist.shape[1], basis_in.shape[2], clusters
    blocks = waves // GROUP
    half = blocks // 2
    ends = [blocks * cut // CUTS[-1] for cut in CUTS]
    starts = [0] + ends[:-1]

    loads = [
        pltpu.make_async_copy(own, raw, local_sem.at[0]),
        pltpu.make_async_copy(fine_in.at[f], fine, local_sem.at[1]),
        pltpu.make_async_copy(coarse_in, coarse, local_sem.at[2]),
        pltpu.make_async_copy(in_in, basis_in, local_sem.at[3]),
        pltpu.make_async_copy(couple_in.at[0], couple, local_sem.at[4]),
        pltpu.make_async_copy(out_in, basis_out, local_sem.at[5]),
    ]
    share = waves // LOADS
    chunks = [
        pltpu.make_async_copy(
            near_in.at[0, :, pl.ds(w * share, share)], near.at[:, pl.ds(w * share, share)], near_sem.at[w]
        )
        for w in range(LOADS)
    ]

    barrier = pltpu.get_barrier_semaphore()
    for peer in peers:
        pl.semaphore_signal(barrier, inc=1, device_id=(peer, c), device_id_type=MESH)
    pl.semaphore_signal(barrier, inc=1, device_id=(f, partner), device_id_type=MESH)

    def when(flag, action):
        @pl.when(flag)
        def _():
            action()

    when(has_up, lambda: pl.semaphore_signal(barrier, inc=1, device_id=(f, up), device_id_type=MESH))
    when(has_down, lambda: pl.semaphore_signal(barrier, inc=1, device_id=(f, down), device_id_type=MESH))
    for copy in loads[:3]:
        copy.start()

    sent = []

    def give(peer, slot, e, number):
        return pltpu.make_async_remote_copy(
            src_ref=hist.at[slot, e], dst_ref=hist.at[slot, e],
            send_sem=hist_send.at[number, e], recv_sem=hist_recv.at[slot, e],
            device_id=(peer, c), device_id_type=MESH,
        )

    def arrived(slot, e):
        give(peers[0], slot, e, 0).wait_recv()

    def send(*what):
        sent.append(give(*what))
        sent[-1].start()

    def turn(g):
        for e in (2 * g, 2 * g + 1):
            hist[f, e] = wide[pl.ds(e, hist.shape[2], stride=exc), :].astype(jnp.bfloat16)

    def give_part(g, i):
        for number, peer in enumerate(peers):
            send(peer, f, 2 * g + (i + number) % 2, number)

    def relay_pair(g):
        if square:
            arrived(beside, 2 * g)
            send(across, beside, 2 * g, len(peers))
            arrived(across, 2 * g + 1)
            send(beside, across, 2 * g + 1, len(peers))

    def finish_pair(g):
        if square:
            corner = (beside + 2) % freqs
            order = [(beside, 1), (across, 0), (corner, 0), (corner, 1)]
        else:
            order = [(peer, part) for peer in peers for part in range(2)]
        for slot, part in order:
            arrived(slot, 2 * g + part)

    units = [pre[0][0], pre[0][1], pre[1][0], pre[1][1]] + list(post)

    def pass_on(u, source, target, way):
        return pltpu.make_async_remote_copy(
            src_ref=units[u].at[source], dst_ref=units[u].at[source],
            send_sem=send_sem.at[u % KEEP, source // 2, way], recv_sem=recv_sem.at[u, source],
            device_id=(f, target), device_id_type=MESH,
        )

    state = {"own": 0}

    def send_own():
        u = state["own"]
        drain(u - KEEP)
        when(has_up, lambda: pass_on(u, c, up, 0).start())
        when(has_down, lambda: pass_on(u, c, down, 1).start())
        pass_on(u, c, partner, 2).start()
        state["own"] += 1

    def relay(u, d):
        below, above = c - 2 * d, c + 2 * d

        def from_below():
            pass_on(u, below, partner, 2).wait_recv()
            when(has_up, lambda: pass_on(u, below, up, 0).start())
            pass_on(u, below, partner, 2).start()

        def from_above():
            pass_on(u, above, partner, 2).wait_recv()
            when(has_down, lambda: pass_on(u, above, down, 1).start())
            pass_on(u, above, partner, 2).start()

        when(z >= d, from_below)
        when(z + d < levels, from_above)

    passed = set()

    def pass_unit(u, *hops):
        for d in hops:
            if d < levels and (u, d) not in passed:
                assert u < state["own"]
                passed.add((u, d))
                relay(u, d)

    def pump(tick):
        for t in range(1, tick + 1):
            for d in range(levels - 1, 0, -1):
                if 0 <= t - d < len(units):
                    pass_unit(t - d, d)

    def complete(u):
        pass_unit(u, *range(1, levels))
        pass_on(u, partner, partner, 2).wait_recv()
        for d in range(1, levels):
            below, above = partner - 2 * d, partner + 2 * d
            when(z >= d, lambda: pass_on(u, below, partner, 2).wait_recv())
            when(z + d < levels, lambda: pass_on(u, above, partner, 2).wait_recv())

    def make(g, p):
        value = transform(g, p, hist, table)
        if g < 2:
            pre[g][p][c] = value
            return
        for w in range(parts):
            if p * half <= starts[w] < (p + 1) * half:
                post[w][c, g - 2] = value[starts[w] - p * half : ends[w] - p * half]

    def compress(w):
        p = starts[w] // half
        lane = lax.broadcasted_iota(jnp.int32, (exc, LANES), 1) // rank

        count = ends[w] - starts[w]
        unroll = math.gcd(count, UNROLL)

        def step(turn, carry):
            pairs = []
            for n in range(unroll):
                i = turn * unroll + n
                b = starts[w] - p * half + i
                left = jnp.concatenate([pre[0][p][c, b], pre[1][p][c, b], post[w][c, 0, i], post[w][c, 1, i]], 0)
                first = (starts[w] + i) * GROUP
                right = [basis_in[pl.ds(first, GROUP), part].reshape(GROUP * rank, panels) for part in range(2)]
                pairs.append(pairs_of(dot(left, jnp.concatenate(right, 0), NT), GROUP * rank))
            for n, pair in enumerate(pairs):
                for part in range(2):
                    spread[n, part] = pair[part]
            for n in range(unroll):
                outs = []
                for part in range(2):
                    rows = spread[n, part, pl.ds(0, exc, stride=GROUP), :]
                    for k in range(1, GROUP):
                        rows = jnp.where(lane == k, spread[n, part, pl.ds(k, exc, stride=GROUP), :], rows)
                    outs.append(rows)
                post[w][c, 2, turn * unroll + n] = jnp.concatenate(outs, 0).astype(jnp.bfloat16)
            return carry

        lax.fori_loop(0, count // unroll, step, 0)

    def set_limits():
        width = sources * rank
        source = lax.broadcasted_iota(jnp.int32, (sources, width), 1) // rank
        keep = source == lax.broadcasted_iota(jnp.int32, (sources, width), 0)
        for j in range(slots):
            keep = keep & (source != near_list[j, c])
        turned = jnp.transpose(ranks[...].astype(jnp.float32)).astype(jnp.bfloat16)
        top = dot(turned, jnp.where(keep, 1.0, 0.0).astype(jnp.bfloat16), NN)
        within = (lax.broadcasted_iota(jnp.int32, top.shape, 1) % rank).astype(jnp.float32)
        limit[...] = jnp.where(within < top, top, 0.0)

    def far_part(w):
        count = ends[w] - starts[w]
        unroll = math.gcd(count, 2)
        rows = 2 * exc
        position = lax.broadcasted_iota(jnp.int32, (rank, sources * rank), 0).astype(jnp.float32)

        def step(pair, carry):
            local = [pair * unroll + u for u in range(unroll)]
            members = [((starts[w] + b) * GROUP + i, i, u) for u, b in enumerate(local) for i in range(GROUP)]
            packed = [[post[w][s, 2, b].astype(jnp.float32) for s in range(sources)] for b in local]
            stacked = [
                jnp.concatenate([v[:, i * rank : (i + 1) * rank] for v in packed[u]], axis=1).astype(jnp.bfloat16)
                for _, i, u in members
            ]
            mixes = []
            for (wave, _, _), left in zip(members, stacked):
                keep = position < limit[pl.ds(wave, 1), :]
                views = [couple[wave, part] for part in range(2)]
                mixes.append([dot(left, jnp.where(keep, v, jnp.zeros_like(v)), NT) for v in views])
            mixed = [
                jnp.concatenate([r[:exc] - m[exc:], r[exc:] + m[:exc]], 0).astype(jnp.bfloat16) for r, m in mixes
            ]
            sums = [[dot(m, basis_out[wave, part], NN) for part in range(2)] for (wave, _, _), m in zip(members, mixed)]
            for (wave, _, _), (r, m) in zip(members, sums):
                far[wave, pl.ds(0, exc)] = r[:exc] - m[exc:]
                far[wave, pl.ds(exc, rows - exc)] = r[exc:] + m[:exc]
            return carry

        lax.fori_loop(0, count // unroll, step, 0)

    picked = [near_list[j, c] for j in range(slots)]

    def near_part(w):
        p = starts[w] // half
        mine = lax.broadcasted_iota(jnp.int32, (GROUP * exc, panels), 0) % GROUP

        count = ends[w] - starts[w]
        unroll = math.gcd(count, 2)

        def step(turn, carry):
            totals = []
            for n in range(unroll):
                i = turn * unroll + n
                b = starts[w] - p * half + i
                views = [[pre[0][p][s, b], pre[1][p][s, b], post[w][s, 0, i], post[w][s, 1, i]] for s in picked]
                left = jnp.concatenate([jnp.concatenate(v, 0) for v in views], 1)
                first = (starts[w] + i) * GROUP
                total = None
                for k in range(GROUP):
                    right = [near[j, first + k].reshape(2 * panels, panels) for j in range(slots)]
                    pair = pairs_of(dot(left, jnp.concatenate(right, 1), NT), panels)
                    total = pair if total is None else [jnp.where(mine == k, v, t) for v, t in zip(pair, total)]
                totals.append(total)
            for n, total in enumerate(totals):
                first = (starts[w] + turn * unroll + n) * GROUP
                for part in range(2):
                    spread[n, part] = total[part]
                for k in range(GROUP):
                    for part in range(2):
                        rows = spread[n, part, pl.ds(k, exc, stride=GROUP), :]
                        out[first + k, part] = (rows + far[first + k, pl.ds(part * exc, exc)]).astype(out.dtype)
            return carry

        lax.fori_loop(0, count // unroll, step, 0)

    def deliver(w):
        span = pl.ds(starts[w] * GROUP, (ends[w] - starts[w]) * GROUP)
        return pltpu.make_async_copy(out.at[span], result.at[span], out_sem.at[w])

    drained = set()

    def drain(u):
        if u < 0 or u in drained:
            return
        drained.add(u)
        pass_unit(u, *range(1, levels))
        when(has_up, lambda: pass_on(u, c, up, 0).wait_send())
        when(has_down, lambda: pass_on(u, c, down, 1).wait_send())
        pass_on(u, c, partner, 2).wait_send()
        for d in range(1, levels):
            below, above = c - 2 * d, c + 2 * d

            def below_sent():
                when(has_up, lambda: pass_on(u, below, up, 0).wait_send())
                pass_on(u, below, partner, 2).wait_send()

            def above_sent():
                when(has_down, lambda: pass_on(u, above, down, 1).wait_send())
                pass_on(u, above, partner, 2).wait_send()

            when(z >= d, below_sent)
            when(z + d < levels, above_sent)

    loads[0].wait()
    wide[...] = raw[...].astype(jnp.float32).reshape(wide.shape)
    turn(0)
    pl.semaphore_wait(barrier, len(peers) + 1 + jnp.where(z + 1 < levels, 1, 0) + jnp.where(z > 0, 1, 0))
    give_part(0, 0)
    for g in range(1, exc // 2):
        turn(g)
    for copy in loads[1:3]:
        copy.wait()
    fill_tables(coarse, fine, table)
    set_limits()
    give_part(0, 1)
    for copy in loads[3:] + chunks:
        copy.start()

    def give_pair(g):
        give_part(g, 0)
        give_part(g, 1)

    def make_pair(g):
        for p in range(2):
            make(g, p)
            if g < 2:
                send_own()

    relay_pair(0)
    give_pair(1)
    finish_pair(0)
    make_pair(0)
    relay_pair(1)
    give_pair(2)
    finish_pair(1)
    make_pair(1)
    relay_pair(2)
    give_pair(3)
    pass_unit(0, 1)
    pass_unit(1, 1)
    finish_pair(2)
    make_pair(2)
    relay_pair(3)
    pass_unit(0, 2)
    pass_unit(2, 1)
    pass_unit(1, 2)
    pass_unit(3, 1)
    finish_pair(3)
    make_pair(3)
    loads[3].wait()
    compress(0)
    send_own()
    pass_unit(2, 2)
    pass_unit(3, 2)
    compress(1)
    pass_unit(0, 3)
    pass_unit(1, 3)
    pass_unit(4, 1)
    send_own()
    compress(2)
    for copy in sent:
        copy.wait_send()
    pass_unit(4, 2)
    pass_unit(5, 1)
    send_own()
    pass_unit(2, 3)
    pass_unit(3, 3)
    for w in range(3, parts):
        compress(w)
    for copy in loads[4:]:
        copy.wait()
    ready = 0
    for w in range(parts):
        pump(6 + w)
        if state["own"] < len(units):
            send_own()
        complete(4 + w)
        far_part(w)
        pump(7 + w)
        if 5 + w < len(units):
            pass_unit(5 + w, *range(1, levels))
        drain(w)
        while ready < LOADS and ready * share < ends[w] * GROUP:
            chunks[ready].wait()
            ready += 1
        if starts[w] % half == 0:
            for g in range(2):
                complete(2 * g + starts[w] // half)
        near_part(w)
        deliver(w).start()
    for u in range(len(units)):
        drain(u)
    for w in range(parts):
        deliver(w).wait()


def local(history, near_blocks, near_list, basis_out, basis_in, coupling, ranks):
    length, exc, panels = history.shape
    waves, _, rank, _ = basis_in.shape
    clusters = lax.axis_size("clus")
    freqs = lax.axis_size("freq")
    slots = near_blocks.shape[1]
    total = length * freqs
    blocks = waves // GROUP
    half = blocks // 2
    rows = 2 * exc
    bf16, f32 = jnp.bfloat16, jnp.float32
    fine, coarse = wave_constants(freqs, waves, total)
    ends = [blocks * cut // CUTS[-1] for cut in CUTS]
    sizes = [b - a for a, b in zip([0] + ends[:-1], ends)]
    vmem, anywhere = pl.BlockSpec(memory_space=pltpu.VMEM), pl.BlockSpec(memory_space=pl.ANY)
    dma = pltpu.SemaphoreType.DMA
    units = 4 + len(CUTS)
    return pl.pallas_call(
        functools.partial(kernel, freqs, clusters),
        out_shape=jax.ShapeDtypeStruct((waves, 2, exc, panels), bf16),
        in_specs=[pl.BlockSpec(memory_space=pltpu.SMEM), vmem] + [anywhere] * 7,
        out_specs=anywhere,
        scratch_shapes=[
            pltpu.VMEM((waves, 2, exc, panels), bf16),
            pltpu.VMEM(history.shape, bf16),
            pltpu.VMEM((length * exc, panels), f32),
            pltpu.VMEM((freqs, exc, length, panels), bf16),
            pltpu.VMEM(fine.shape[1:], f32),
            pltpu.VMEM(coarse.shape, f32),
            pltpu.VMEM((2, 2 * waves, total), bf16),
            pltpu.VMEM(near_blocks.shape[1:], bf16),
            pltpu.VMEM(coupling.shape[1:], bf16),
            pltpu.VMEM(basis_out.shape, bf16),
            pltpu.VMEM(basis_in.shape, bf16),
            pltpu.VMEM((waves, clusters * rank), f32),
            pltpu.VMEM((waves, rows, panels), f32),
            pltpu.VMEM((UNROLL, 2, GROUP * exc, panels), f32),
        ]
        + [pltpu.VMEM((clusters, half, 4 * GROUP, panels), bf16)] * 4
        + [pltpu.VMEM((clusters, 3, size, 4 * GROUP, panels), bf16) for size in sizes]
        + [
            dma((6,)),
            dma((LOADS,)),
            dma((len(CUTS),)),
            dma((3 if freqs == 4 else freqs, exc)),
            dma((freqs, exc)),
            dma((KEEP, clusters // 2, 3)),
            dma((units, clusters)),
        ],
        compiler_params=pltpu.CompilerParams(
            collective_id=0, has_side_effects=True, vmem_limit_bytes=60 * 1024 * 1024
        ),
    )(near_list.T, ranks[0].T, fine, coarse, history, near_blocks, coupling, basis_out, basis_in)


def solution(mesh):
    placed = (
        P("freq", None, "clus"),
        P("clus", None, "freq", None, None, None),
        P(),
        P("freq", None, None, "clus"),
        P("freq", None, None, "clus"),
        P("clus", "freq", None, None, None),
        P("clus", "freq", None),
    )
    return jax.shard_map(
        local, mesh=mesh, in_specs=placed, out_specs=P("freq", None, None, "clus"), check_vma=False
    )
```
